1024 devices in a mesh: dp: 256 (over x, z, core), col: 4 (over y).
Axes of the slice: x: 4, y: 4, z: 32, core: 2. Of those that a mesh axis runs over, the one named last changes fastest.
Arguments:
- queries: bfloat16 [1024, 2048], P('dp'), may hold values from -6 to 6
- kernel_inv: bfloat16 [2048, 2048], P(None, 'col'), may hold values from -0.125 to 0.125
- train_grads: bfloat16 [262144, 2048], P('dp'), may hold values from -0.125 to 0.125
- candidates: int32 [1024, 128], replicated, may hold values from 0 to 255, all different within a row
- block_slot: int32 [256], replicated, may hold values from 0 to 255, each once
Outputs:
- scores: bfloat16 [1024, 262144], P('col', 'dp')
The draws below stay inside these ranges and needn't reach their ends.
Inputs may be any that keep to these rules, and one draw needn't show every extreme that they name: `candidates`: each row names 128 different blocks, and every block is named by some row. `block_slot`: each slot once.
All inputs are finite; a program needn't handle non-finite values.
Results may differ from the reference program's by a relative error of at most 0.0049.
Values may be sent and summed in bfloat16 or wider, within the bound.
A program may use at most 32 MiB of HBM per device.

```python
import jax
import jax.numpy as jnp
from jax import lax

K = 2048
R = 1024
NBLK = 256
Q = 1024
C = 128


def block_levels(key, extent, split, least, largest):
    loudness = 1.0
    for axis_at, parts in split:
        draws = jax.random.uniform(jax.random.fold_in(jax.random.fold_in(key, 6), axis_at), (parts,), jnp.float32, least / len(split), largest / len(split))
        loudness = loudness * jnp.repeat(jnp.exp(draws), extent[axis_at] // parts).reshape((-1,) + (1,) * (len(extent) - 1 - axis_at))
    return loudness


def picks_of(key, rows, number_of, top, lift):
    sequence = jax.random.permutation(jax.random.fold_in(key, 1), number_of)
    boost = sequence
    for power in range(3):
        boost = boost * boost // number_of
    boost = boost * lift // number_of
    tickets = jax.random.randint(jax.random.fold_in(key, 2), (rows, number_of), 0, 4096) + boost
    holders = jax.random.permutation(jax.random.fold_in(key, 3), rows)[jnp.arange(number_of) % rows]
    tickets = jnp.where(jnp.arange(rows)[:, None] == holders[None, :], 1 << 14, tickets)
    priority = tickets * number_of + jnp.arange(number_of)
    return lax.top_k(priority.astype(jnp.int32), top)[1].astype(jnp.int32)


def noise(rng, shape, spread, reach, split=(), kind=jnp.bfloat16):
    values = spread * jax.random.normal(rng, shape, jnp.float32)
    if split:
        values = values * block_levels(rng, shape, split, -0.22, 0.18)
    return jnp.clip(values, -reach, reach).astype(kind)


def setup_inputs(seed: int = 0) -> dict:
    keys = jax.random.split(jax.random.key(seed), 6)
    return {
        "queries": noise(keys[0], (Q, K), 1.0, 6.0, ((0, 256),)),
        "kernel_inv": noise(keys[1], (K, K), K ** -0.5, 0.125, ((1, 4),)),
        "train_grads": noise(keys[2], (NBLK * R, K), K ** -0.5, 0.125, ((0, 256),)),
        "candidates": picks_of(keys[3], Q, NBLK, C, 8192),
        "block_slot": jax.random.permutation(keys[4], NBLK).astype(jnp.int32),
    }


def reference(queries, kernel_inv, train_grads, candidates, block_slot):
    precond = jnp.dot(queries, kernel_inv, preferred_element_type=jnp.float32).astype(jnp.bfloat16)
    slot_of = jnp.take(block_slot, candidates, axis=0).astype(jnp.int32)
    query_ids = jnp.arange(Q, dtype=jnp.int32)[:, None]
    named = jnp.zeros((Q, NBLK), jnp.float32).at[query_ids, slot_of].set(1.0)
    blocks = train_grads.reshape(NBLK, R, K)

    def one_block(item):
        grads, flags = item
        partial_scores = jnp.dot(precond, grads.T, preferred_element_type=jnp.float32)
        return (partial_scores * flags[:, None]).astype(jnp.bfloat16)

    stacked = lax.map(one_block, (blocks, named.T))
    return jnp.transpose(stacked, (1, 0, 2)).reshape(Q, NBLK * R)
```

```python
import numpy as np
import jax
import jax.numpy as jnp
from jax import lax
from jax.sharding import Mesh, PartitionSpec as P


def listed_flags(candidates, block_slot, first_row, row_count, dp_index):
    owned_rows = lax.dynamic_slice_in_dim(candidates, first_row, row_count, 0)
    numbers = jnp.arange(block_slot.shape[0], dtype=jnp.int32)
    owner = jnp.sum(jnp.where(block_slot == dp_index, numbers, 0))
    flags = jnp.any(owned_rows == owner, axis=1)
    return flags.astype(jnp.float32)


def per_device(queries, kernel_inv, train_grads, candidates, block_slot):
    n_x = lax.axis_size("x")
    n_zc = lax.axis_size("zc")
    n_col = lax.axis_size("col")
    col_index = lax.axis_index("col")
    dp_index = lax.axis_index("x") * n_zc + lax.axis_index("zc")
    per_col = candidates.shape[0] // n_col
    first_row = col_index * per_col
    precond = jnp.dot(queries, kernel_inv, preferred_element_type=jnp.float32).astype(jnp.bfloat16)
    perm = [(a * n_col + b, b * n_col + a) for a in range(n_x) for b in range(n_col)]
    moved = lax.ppermute(precond, ("x", "col"), perm)
    rows = lax.all_gather(moved, "zc", axis=0, tiled=True)
    selected = lax.all_gather(rows, "x", axis=1, tiled=True)
    partial_scores = lax.dot_general(
        selected, train_grads, (((1,), (1,)), ((), ())), preferred_element_type=jnp.float32
    )
    flags = listed_flags(candidates, block_slot, first_row, per_col, dp_index)
    return (partial_scores * flags[:, None]).astype(jnp.bfloat16)


def solution(mesh):
    n_dp, n_col = mesh.devices.shape
    n_x = n_col
    grid = Mesh(mesh.devices.reshape(n_x, n_dp // n_x, n_col), ("x", "zc", "col"))
    rows = ("x", "zc")
    placed = (P(rows, None), P(None, "col"), P(rows, None), P(), P())
    return jax.shard_map(
        per_device, mesh=grid, in_specs=placed, out_specs=P("col", rows), check_vma=False
    )
```

```python
import functools

import jax
import jax.numpy as jnp
from jax import lax
from jax.experimental import pallas as pl
from jax.experimental.pallas import tpu as pltpu
from jax.sharding import Mesh, PartitionSpec as P

MESH = pl.DeviceIdType.MESH


def gather_kernel(n_x, n_zc, block_ref, out_ref, held, send_z, recv_z, send_x, recv_x, own_sem):
    me_x = lax.axis_index("x")
    me_zc = lax.axis_index("zc")
    me_y = lax.axis_index("col")
    width = block_ref.shape[1]
    cols = pl.ds(pl.multiple_of(me_x * width, width), width)

    barrier = pltpu.get_barrier_semaphore()

    def greet(k, carry):
        peer = lax.rem(me_zc + k, n_zc)
        pl.semaphore_signal(barrier, inc=1, device_id=(me_x, peer, me_y), device_id_type=MESH)
        return carry

    lax.fori_loop(1, n_zc, greet, 0)
    for k in range(1, n_x):
        peer = lax.rem(me_x + k, n_x)
        pl.semaphore_signal(barrier, inc=1, device_id=(peer, me_zc, me_y), device_id_type=MESH)
    pl.semaphore_wait(barrier, n_zc - 1 + n_x - 1)

    own = pltpu.make_async_copy(block_ref, held.at[me_zc, :, cols], own_sem)
    own.start()

    def z_copy(src, dst):
        return pltpu.make_async_remote_copy(
            src_ref=block_ref,
            dst_ref=held.at[src, :, cols],
            send_sem=send_z.at[dst],
            recv_sem=recv_z.at[src],
            device_id=(me_x, dst, me_y),
            device_id_type=MESH,
        )

    def z_start(k, carry):
        z_copy(me_zc, lax.rem(me_zc + k, n_zc)).start()
        return carry

    lax.fori_loop(1, n_zc, z_start, 0)
    own.wait()

    def z_arrive(k, carry):
        z_copy(lax.rem(me_zc + k, n_zc), me_zc).wait_recv()
        return carry

    lax.fori_loop(1, n_zc, z_arrive, 0)

    def x_copy(src, dst):
        src_cols = pl.ds(pl.multiple_of(src * width, width), width)
        return pltpu.make_async_remote_copy(
            src_ref=held.at[:, :, src_cols],
            dst_ref=held.at[:, :, src_cols],
            send_sem=send_x.at[dst],
            recv_sem=recv_x.at[src],
            device_id=(dst, me_zc, me_y),
            device_id_type=MESH,
        )

    for k in range(1, n_x):
        x_copy(me_x, lax.rem(me_x + k, n_x)).start()
    for k in range(1, n_x):
        x_copy(lax.rem(me_x + k, n_x), me_x).wait_recv()

    def z_sent(k, carry):
        z_copy(me_zc, lax.rem(me_zc + k, n_zc)).wait_send()
        return carry

    lax.fori_loop(1, n_zc, z_sent, 0)
    for k in range(1, n_x):
        x_copy(me_x, lax.rem(me_x + k, n_x)).wait_send()
    out_ref[...] = held[...]


def gather_rows(block, n_x, n_zc):
    rows, width = block.shape
    shape = (n_zc, rows, n_x * width)
    return pl.pallas_call(
        functools.partial(gather_kernel, n_x, n_zc),
        out_shape=jax.ShapeDtypeStruct(shape, block.dtype),
        in_specs=[pl.BlockSpec(memory_space=pltpu.VMEM)],
        out_specs=pl.BlockSpec(memory_space=pltpu.VMEM),
        scratch_shapes=[
            pltpu.VMEM(shape, block.dtype),
            pltpu.SemaphoreType.DMA((n_zc,)),
            pltpu.SemaphoreType.DMA((n_zc,)),
            pltpu.SemaphoreType.DMA((n_x,)),
            pltpu.SemaphoreType.DMA((n_x,)),
            pltpu.SemaphoreType.DMA(()),
        ],
        compiler_params=pltpu.CompilerParams(collective_id=0, has_side_effects=True),
        cost_estimate=pl.CostEstimate(
            flops=0, transcendentals=0, bytes_accessed=2 * n_zc * rows * n_x * width * 2
        ),
    )(block)


def listed_flags(candidates, block_slot, first_row, row_count, dp_index):
    owned_rows = lax.dynamic_slice_in_dim(candidates, first_row, row_count, 0)
    numbers = jnp.arange(block_slot.shape[0], dtype=jnp.int32)
    owner = jnp.sum(jnp.where(block_slot == dp_index, numbers, 0))
    flags = jnp.any(owned_rows == owner, axis=1)
    return flags.astype(jnp.float32)


def per_device(queries, kernel_inv, train_grads, candidates, block_slot):
    n_x = lax.axis_size("x")
    n_zc = lax.axis_size("zc")
    n_col = lax.axis_size("col")
    col_index = lax.axis_index("col")
    dp_index = lax.axis_index("x") * n_zc + lax.axis_index("zc")
    per_col = candidates.shape[0] // n_col
    first_row = col_index * per_col
    precond = jnp.dot(queries, kernel_inv, preferred_element_type=jnp.float32).astype(jnp.bfloat16)
    perm = [(a * n_col + b, b * n_col + a) for a in range(n_x) for b in range(n_col)]
    moved = lax.ppermute(precond, ("x", "col"), perm)
    gathered = gather_rows(moved, n_x, n_zc)
    selected = gathered.reshape(per_col, gathered.shape[2])
    partial_scores = lax.dot_general(
        selected, train_grads, (((1,), (1,)), ((), ())), preferred_element_type=jnp.float32
    )
    flags = listed_flags(candidates, block_slot, first_row, per_col, dp_index)
    return (partial_scores * flags[:, None]).astype(jnp.bfloat16)


def solution(mesh):
    n_dp, n_col = mesh.devices.shape
    n_x = n_col
    grid = Mesh(mesh.devices.reshape(n_x, n_dp // n_x, n_col), ("x", "zc", "col"))
    rows = ("x", "zc")
    placed = (P(rows, None), P(None, "col"), P(rows, None), P(), P())
    return jax.shard_map(
        per_device, mesh=grid, in_specs=placed, out_specs=P("col", rows), check_vma=False
    )
```

```python
import functools

import jax
import jax.numpy as jnp
from jax import lax
from jax.experimental import pallas as pl
from jax.experimental.pallas import tpu as pltpu
from jax.sharding import Mesh, PartitionSpec as P

MESH = pl.DeviceIdType.MESH


def gather_kernel(n_x, n_z, block_ref, out_ref, held, send_ring, recv_ring, send_pair, recv_pair,
                  send_x, recv_x, own_sem):
    me_x = lax.axis_index("x")
    me_zc = lax.axis_index("zc")
    me_y = lax.axis_index("col")
    me_z = me_zc // 2
    lane = me_zc % 2
    width = block_ref.shape[1]
    cols = pl.ds(pl.multiple_of(me_x * width, width), width)
    reach = (n_z // 2, (n_z - 1) // 2)
    nexts = (lax.rem(me_z + 1, n_z) * 2 + lane, lax.rem(me_z + n_z - 1, n_z) * 2 + lane)
    pair = me_z * 2 + 1 - lane
    x_peers = [(k, lax.rem(me_x + k, n_x)) for k in range(1, n_x)]

    barrier = pltpu.get_barrier_semaphore()
    peers = [(me_x, nexts[0], me_y), (me_x, nexts[1], me_y), (me_x, pair, me_y)]
    peers += [(px, me_z * 2 + other, me_y) for _, px in x_peers for other in range(2)]
    for peer in peers:
        pl.semaphore_signal(barrier, inc=1, device_id=peer, device_id_type=MESH)
    pl.semaphore_wait(barrier, len(peers))

    own = pltpu.make_async_copy(block_ref, held.at[me_zc, :, cols], own_sem)
    own.start()

    def slot_of(way, hops):
        origin = me_z - hops if way == 0 else me_z + hops
        return lax.rem(origin + n_z, n_z) * 2 + lane

    def ring_copy(way, step, source, slot):
        return pltpu.make_async_remote_copy(
            src_ref=source, dst_ref=held.at[slot, :, cols],
            send_sem=send_ring.at[way, step], recv_sem=recv_ring.at[way, step],
            device_id=(me_x, nexts[way], me_y), device_id_type=MESH)

    def spread(source, slot):
        dst = held.at[slot, :, cols]
        pltpu.make_async_remote_copy(
            src_ref=source, dst_ref=dst, send_sem=send_pair, recv_sem=recv_pair,
            device_id=(me_x, pair, me_y), device_id_type=MESH).start()
        for k, px in x_peers:
            for other in range(2):
                pltpu.make_async_remote_copy(
                    src_ref=source, dst_ref=dst, send_sem=send_x.at[k, other],
                    recv_sem=recv_x.at[n_x - k, lane],
                    device_id=(px, me_z * 2 + other, me_y), device_id_type=MESH).start()

    for way in range(2):
        if reach[way] >= 1:
            ring_copy(way, 1, block_ref, me_zc).start()
    spread(block_ref, me_zc)

    def step_body(step, ways, forward):
        for way in ways:
            slot = slot_of(way, step)
            ring_copy(way, step, held.at[slot, :, cols], slot).wait_recv()
            if forward[way]:
                ring_copy(way, step + 1, held.at[slot, :, cols], slot).start()
        for way in ways:
            slot = slot_of(way, step)
            spread(held.at[slot, :, cols], slot)

    def both(step, carry):
        step_body(step, (0, 1), (True, True))
        return carry

    lax.fori_loop(1, reach[1], both, 0)
    if reach[1] >= 1:
        step_body(reach[1], (0, 1), (reach[1] < reach[0], False))
    if reach[0] > reach[1]:
        step_body(reach[0], (0,), (False, False))

    for way in range(2):
        for step in range(1, reach[way] + 1):
            slot = slot_of(way, step - 1)
            ring_copy(way, step, held.at[slot, :, cols], slot).wait_send()
    line = held.at[pl.ds(0, n_z), :, cols]
    pltpu.make_async_remote_copy(
        src_ref=line, dst_ref=line, send_sem=send_pair, recv_sem=recv_pair,
        device_id=(me_x, pair, me_y), device_id_type=MESH).wait()
    for k, px in x_peers:
        for other in range(2):
            pltpu.make_async_remote_copy(
                src_ref=line, dst_ref=line, send_sem=send_x.at[k, other], recv_sem=recv_x.at[k, other],
                device_id=(px, me_z * 2 + other, me_y), device_id_type=MESH).wait()
    own.wait()
    out_ref[...] = held[...]


def gather_rows(block, n_x, n_zc):
    rows, width = block.shape
    n_z = n_zc // 2
    shape = (n_zc, rows, n_x * width)
    return pl.pallas_call(
        functools.partial(gather_kernel, n_x, n_z),
        out_shape=jax.ShapeDtypeStruct(shape, block.dtype),
        in_specs=[pl.BlockSpec(memory_space=pltpu.VMEM)],
        out_specs=pl.BlockSpec(memory_space=pltpu.VMEM),
        scratch_shapes=[
            pltpu.VMEM(shape, block.dtype),
            pltpu.SemaphoreType.DMA((2, n_z // 2 + 1)),
            pltpu.SemaphoreType.DMA((2, n_z // 2 + 1)),
            pltpu.SemaphoreType.DMA(()),
            pltpu.SemaphoreType.DMA(()),
            pltpu.SemaphoreType.DMA((n_x, 2)),
            pltpu.SemaphoreType.DMA((n_x, 2)),
            pltpu.SemaphoreType.DMA(()),
        ],
        compiler_params=pltpu.CompilerParams(collective_id=0, has_side_effects=True),
        cost_estimate=pl.CostEstimate(
            flops=0, transcendentals=0, bytes_accessed=2 * n_zc * rows * n_x * width * 2
        ),
    )(block)


def listed_flags(candidates, block_slot, first_row, row_count, dp_index):
    owned_rows = lax.dynamic_slice_in_dim(candidates, first_row, row_count, 0)
    numbers = jnp.arange(block_slot.shape[0], dtype=jnp.int32)
    owner = jnp.sum(jnp.where(block_slot == dp_index, numbers, 0))
    flags = jnp.any(owned_rows == owner, axis=1)
    return flags.astype(jnp.float32)


def per_device(queries, kernel_inv, train_grads, candidates, block_slot):
    n_x = lax.axis_size("x")
    n_zc = lax.axis_size("zc")
    n_col = lax.axis_size("col")
    col_index = lax.axis_index("col")
    dp_index = lax.axis_index("x") * n_zc + lax.axis_index("zc")
    per_col = candidates.shape[0] // n_col
    first_row = col_index * per_col
    precond = jnp.dot(queries, kernel_inv, preferred_element_type=jnp.float32).astype(jnp.bfloat16)
    perm = [(a * n_col + b, b * n_col + a) for a in range(n_x) for b in range(n_col)]
    moved = lax.ppermute(precond, ("x", "col"), perm)
    gathered = gather_rows(moved, n_x, n_zc)
    selected = gathered.reshape(per_col, gathered.shape[2])
    partial_scores = lax.dot_general(
        selected, train_grads, (((1,), (1,)), ((), ())), preferred_element_type=jnp.float32
    )
    flags = listed_flags(candidates, block_slot, first_row, per_col, dp_index)
    return (partial_scores * flags[:, None]).astype(jnp.bfloat16)


def solution(mesh):
    n_dp, n_col = mesh.devices.shape
    n_x = n_col
    grid = Mesh(mesh.devices.reshape(n_x, n_dp // n_x, n_col), ("x", "zc", "col"))
    rows = ("x", "zc")
    placed = (P(rows, None), P(None, "col"), P(rows, None), P(), P())
    return jax.shard_map(
        per_device, mesh=grid, in_specs=placed, out_specs=P("col", rows), check_vma=False
    )
```

```python
import functools

import jax
import jax.numpy as jnp
from jax import lax
from jax.experimental import pallas as pl
from jax.experimental.pallas import tpu as pltpu
from jax.sharding import Mesh, PartitionSpec as P

MESH = pl.DeviceIdType.MESH


def gather_kernel(n_x, n_z, block_ref, out_ref, held, send_z, recv_z, send_x, recv_x, send_pair,
                  recv_pair, own_sem):
    me_x = lax.axis_index("x")
    me_zc = lax.axis_index("zc")
    me_y = lax.axis_index("col")
    me_z = me_zc // 2
    lane = me_zc % 2
    pair = me_z * 2 + 1 - lane
    z_peers = [(k, lax.rem(me_z + k, n_z) * 2 + lane) for k in range(1, n_z)]
    x_peers = [(k, lax.rem(me_x + k, n_x)) for k in range(1, n_x)]

    barrier = pltpu.get_barrier_semaphore()
    peers = [(me_x, zc, me_y) for _, zc in z_peers] + [(px, me_zc, me_y) for _, px in x_peers]
    peers.append((me_x, pair, me_y))
    for peer in peers:
        pl.semaphore_signal(barrier, inc=1, device_id=peer, device_id_type=MESH)
    pl.semaphore_wait(barrier, len(peers))

    own = pltpu.make_async_copy(block_ref, held.at[me_x, lane, me_z], own_sem)
    own.start()

    def z_copy(k, zc):
        return pltpu.make_async_remote_copy(
            src_ref=block_ref, dst_ref=held.at[me_x, lane, me_z],
            send_sem=send_z.at[k], recv_sem=recv_z.at[n_z - k],
            device_id=(me_x, zc, me_y), device_id_type=MESH)

    for k, zc in z_peers:
        z_copy(k, zc).start()
    for k, zc in z_peers:
        src_z = lax.rem(me_z + k, n_z)
        pltpu.make_async_remote_copy(
            src_ref=block_ref, dst_ref=held.at[me_x, lane, src_z],
            send_sem=send_z.at[k], recv_sem=recv_z.at[k],
            device_id=(me_x, zc, me_y), device_id_type=MESH).wait_recv()
    own.wait()

    def to_pair(c, index):
        line = held.at[c, lane]
        return pltpu.make_async_remote_copy(
            src_ref=line, dst_ref=line, send_sem=send_pair.at[index], recv_sem=recv_pair.at[index],
            device_id=(me_x, pair, me_y), device_id_type=MESH)

    def x_copy(k, px):
        line = held.at[me_x, lane]
        return pltpu.make_async_remote_copy(
            src_ref=line, dst_ref=line, send_sem=send_x.at[k], recv_sem=recv_x.at[n_x - k],
            device_id=(px, me_zc, me_y), device_id_type=MESH)

    to_pair(me_x, 0).start()
    for k, px in x_peers:
        x_copy(k, px).start()
    for k, px in x_peers:
        line = held.at[px, lane]
        pltpu.make_async_remote_copy(
            src_ref=line, dst_ref=line, send_sem=send_x.at[k], recv_sem=recv_x.at[k],
            device_id=(px, me_zc, me_y), device_id_type=MESH).wait_recv()
        to_pair(px, k).start()

    for index in range(n_x):
        c = me_x if index == 0 else x_peers[index - 1][1]
        line = held.at[c, 1 - lane]
        pltpu.make_async_remote_copy(
            src_ref=line, dst_ref=line, send_sem=send_pair.at[index], recv_sem=recv_pair.at[index],
            device_id=(me_x, pair, me_y), device_id_type=MESH).wait_recv()

    for k, zc in z_peers:
        z_copy(k, zc).wait_send()
    for k, px in x_peers:
        x_copy(k, px).wait_send()
    to_pair(me_x, 0).wait_send()
    for k, px in x_peers:
        to_pair(px, k).wait_send()
    out_ref[...] = held[...]


def gather_rows(block, n_x, n_zc):
    n_z = n_zc // 2
    shape = (n_x, 2, n_z) + block.shape
    return pl.pallas_call(
        functools.partial(gather_kernel, n_x, n_z),
        out_shape=jax.ShapeDtypeStruct(shape, block.dtype),
        in_specs=[pl.BlockSpec(memory_space=pltpu.VMEM)],
        out_specs=pl.BlockSpec(memory_space=pltpu.VMEM),
        scratch_shapes=[
            pltpu.VMEM(shape, block.dtype),
            pltpu.SemaphoreType.DMA((n_z,)),
            pltpu.SemaphoreType.DMA((n_z,)),
            pltpu.SemaphoreType.DMA((n_x,)),
            pltpu.SemaphoreType.DMA((n_x,)),
            pltpu.SemaphoreType.DMA((n_x,)),
            pltpu.SemaphoreType.DMA((n_x,)),
            pltpu.SemaphoreType.DMA(()),
        ],
        compiler_params=pltpu.CompilerParams(collective_id=0, has_side_effects=True),
        cost_estimate=pl.CostEstimate(
            flops=0, transcendentals=0, bytes_accessed=2 * n_x * n_zc * block.size * 2
        ),
    )(block)


def listed_flags(candidates, block_slot, first_row, row_count, dp_index):
    owned_rows = lax.dynamic_slice_in_dim(candidates, first_row, row_count, 0)
    numbers = jnp.arange(block_slot.shape[0], dtype=jnp.int32)
    owner = jnp.sum(jnp.where(block_slot == dp_index, numbers, 0))
    flags = jnp.any(owned_rows == owner, axis=1)
    return flags.astype(jnp.float32)


def per_device(queries, kernel_inv, train_grads, candidates, block_slot):
    n_x = lax.axis_size("x")
    n_zc = lax.axis_size("zc")
    n_col = lax.axis_size("col")
    col_index = lax.axis_index("col")
    dp_index = lax.axis_index("x") * n_zc + lax.axis_index("zc")
    per_col = candidates.shape[0] // n_col
    first_row = col_index * per_col
    precond = jnp.dot(queries, kernel_inv, preferred_element_type=jnp.float32).astype(jnp.bfloat16)
    perm = [(a * n_col + b, b * n_col + a) for a in range(n_x) for b in range(n_col)]
    rows, width = precond.shape
    tile = precond.reshape(rows * width // 128, 128)
    moved = lax.ppermute(tile, ("x", "col"), perm)
    held = gather_rows(moved, n_x, n_zc)
    held = held.reshape(n_x, 2, n_zc // 2, rows, width // 128, 128)
    selected = jnp.transpose(held, (2, 1, 3, 0, 4, 5)).reshape(per_col, n_x * width)
    partial_scores = lax.dot_general(
        selected, train_grads, (((1,), (1,)), ((), ())), preferred_element_type=jnp.float32
    )
    flags = listed_flags(candidates, block_slot, first_row, per_col, dp_index)
    return (partial_scores * flags[:, None]).astype(jnp.bfloat16)


def solution(mesh):
    n_dp, n_col = mesh.devices.shape
    n_x = n_col
    grid = Mesh(mesh.devices.reshape(n_x, n_dp // n_x, n_col), ("x", "zc", "col"))
    rows = ("x", "zc")
    placed = (P(rows, None), P(None, "col"), P(rows, None), P(), P())
    return jax.shard_map(
        per_device, mesh=grid, in_specs=placed, out_specs=P("col", rows), check_vma=False
    )
```

```python
import functools

import jax
import jax.numpy as jnp
from jax import lax
from jax.experimental import pallas as pl
from jax.experimental.pallas import tpu as pltpu
from jax.sharding import Mesh, PartitionSpec as P

MESH = pl.DeviceIdType.MESH


def gather_kernel(n_x, n_z, block_ref, cand_ref, slot_ref, out_ref, flags_ref, held, send_z, recv_z,
                  send_x, recv_x, send_pair, recv_pair, own_sem):
    me_x = lax.axis_index("x")
    me_zc = lax.axis_index("zc")
    me_y = lax.axis_index("col")
    me_z = me_zc // 2
    lane = me_zc % 2
    pair = me_z * 2 + 1 - lane
    on_diagonal = me_x == me_y
    z_peers = [(k, lax.rem(me_z + k, n_z) * 2 + lane) for k in range(1, n_z)]
    x_peers = [(k, lax.rem(me_x + k, n_x)) for k in range(1, n_x)]

    barrier = pltpu.get_barrier_semaphore()
    peers = [(me_y, zc, me_x) for _, zc in z_peers] + [(px, me_zc, me_y) for _, px in x_peers]
    peers.append((me_x, pair, me_y))
    for peer in peers:
        pl.semaphore_signal(barrier, inc=1, device_id=peer, device_id_type=MESH)

    @pl.when(jnp.logical_not(on_diagonal))
    def _():
        pl.semaphore_signal(barrier, inc=1, device_id=(me_y, me_zc, me_x), device_id_type=MESH)

    pl.semaphore_wait(barrier, len(peers) + jnp.where(on_diagonal, 0, 1))

    def z_copy(k, zc):
        return pltpu.make_async_remote_copy(
            src_ref=block_ref, dst_ref=held.at[me_y, lane, me_z],
            send_sem=send_z.at[k], recv_sem=recv_z.at[lax.rem(n_z - k, n_z)],
            device_id=(me_y, zc, me_x), device_id_type=MESH)

    for k, zc in z_peers:
        z_copy(k, zc).start()
    own = pltpu.make_async_copy(block_ref, held.at[me_x, lane, me_z], own_sem)

    @pl.when(on_diagonal)
    def _():
        own.start()

    @pl.when(jnp.logical_not(on_diagonal))
    def _():
        z_copy(0, me_zc).start()

    rows = flags_ref.shape[0]
    slots = slot_ref[...]
    number = lax.broadcasted_iota(jnp.int32, slots.shape, 0) * slots.shape[1]
    number = number + lax.broadcasted_iota(jnp.int32, slots.shape, 1)
    owner = jnp.sum(jnp.where(slots == me_x * (2 * n_z) + me_zc, number, 0), keepdims=True)
    listed = cand_ref[pl.ds(pl.multiple_of(me_y * rows, rows), rows), :] == owner
    flags_ref[...] = jnp.max(listed.astype(jnp.float32), axis=1, keepdims=True)

    for k in range(n_z):
        src_z = lax.rem(me_z + k, n_z)
        src_zc = src_z * 2 + lane
        if k == 0:
            @pl.when(on_diagonal)
            def _():
                own.wait()

            @pl.when(jnp.logical_not(on_diagonal))
            def _():
                pltpu.make_async_remote_copy(
                    src_ref=block_ref, dst_ref=held.at[me_x, lane, src_z],
                    send_sem=send_z.at[0], recv_sem=recv_z.at[0],
                    device_id=(me_y, src_zc, me_x), device_id_type=MESH).wait_recv()
        else:
            pltpu.make_async_remote_copy(
                src_ref=block_ref, dst_ref=held.at[me_x, lane, src_z],
                send_sem=send_z.at[k], recv_sem=recv_z.at[k],
                device_id=(me_y, src_zc, me_x), device_id_type=MESH).wait_recv()

    def to_pair(c, index):
        line = held.at[c, lane]
        return pltpu.make_async_remote_copy(
            src_ref=line, dst_ref=line, send_sem=send_pair.at[index], recv_sem=recv_pair.at[index],
            device_id=(me_x, pair, me_y), device_id_type=MESH)

    def x_copy(k, px):
        line = held.at[me_x, lane]
        return pltpu.make_async_remote_copy(
            src_ref=line, dst_ref=line, send_sem=send_x.at[k], recv_sem=recv_x.at[n_x - k],
            device_id=(px, me_zc, me_y), device_id_type=MESH)

    to_pair(me_x, 0).start()
    for k, px in x_peers:
        x_copy(k, px).start()
    for k, px in x_peers:
        line = held.at[px, lane]
        pltpu.make_async_remote_copy(
            src_ref=line, dst_ref=line, send_sem=send_x.at[k], recv_sem=recv_x.at[k],
            device_id=(px, me_zc, me_y), device_id_type=MESH).wait_recv()
        to_pair(px, k).start()

    for index in range(n_x):
        c = me_x if index == 0 else x_peers[index - 1][1]
        line = held.at[c, 1 - lane]
        pltpu.make_async_remote_copy(
            src_ref=line, dst_ref=line, send_sem=send_pair.at[index], recv_sem=recv_pair.at[index],
            device_id=(me_x, pair, me_y), device_id_type=MESH).wait_recv()

    for k, zc in z_peers:
        z_copy(k, zc).wait_send()

    @pl.when(jnp.logical_not(on_diagonal))
    def _():
        z_copy(0, me_zc).wait_send()

    for k, px in x_peers:
        x_copy(k, px).wait_send()
    to_pair(me_x, 0).wait_send()
    for k, px in x_peers:
        to_pair(px, k).wait_send()
    out_ref[...] = held[...]


def gather_rows(block, candidates, block_slot, n_x, n_zc, rows):
    n_z = n_zc // 2
    shape = (n_x, 2, n_z) + block.shape
    slots = block_slot.reshape(-1, 128) if block_slot.size % 128 == 0 else block_slot.reshape(1, -1)
    return pl.pallas_call(
        functools.partial(gather_kernel, n_x, n_z),
        out_shape=(
            jax.ShapeDtypeStruct(shape, block.dtype),
            jax.ShapeDtypeStruct((rows, 1), jnp.float32),
        ),
        in_specs=[pl.BlockSpec(memory_space=pltpu.VMEM)] * 3,
        out_specs=(pl.BlockSpec(memory_space=pltpu.VMEM), pl.BlockSpec(memory_space=pltpu.VMEM)),
        scratch_shapes=[
            pltpu.VMEM(shape, block.dtype),
            pltpu.SemaphoreType.DMA((n_z,)),
            pltpu.SemaphoreType.DMA((n_z,)),
            pltpu.SemaphoreType.DMA((n_x,)),
            pltpu.SemaphoreType.DMA((n_x,)),
            pltpu.SemaphoreType.DMA((n_x,)),
            pltpu.SemaphoreType.DMA((n_x,)),
            pltpu.SemaphoreType.DMA(()),
        ],
        compiler_params=pltpu.CompilerParams(collective_id=0, has_side_effects=True),
        cost_estimate=pl.CostEstimate(
            flops=0, transcendentals=0, bytes_accessed=2 * n_x * n_zc * block.size * 2
        ),
    )(block, candidates, slots)


def per_device(queries, kernel_inv, train_grads, candidates, block_slot):
    n_x = lax.axis_size("x")
    n_zc = lax.axis_size("zc")
    n_col = lax.axis_size("col")
    per_col = candidates.shape[0] // n_col
    precond = jnp.dot(queries, kernel_inv, preferred_element_type=jnp.float32).astype(jnp.bfloat16)
    rows, width = precond.shape
    tile = precond.reshape(rows * width // 128, 128)
    held, flags = gather_rows(tile, candidates, block_slot, n_x, n_zc, per_col)
    held = held.reshape(n_x, 2, n_zc // 2, rows, width // 128, 128)
    selected = jnp.transpose(held, (2, 1, 3, 0, 4, 5)).reshape(per_col, n_x * width)
    partial_scores = lax.dot_general(
        selected, train_grads, (((1,), (1,)), ((), ())), preferred_element_type=jnp.float32
    )
    return (partial_scores * flags).astype(jnp.bfloat16)


def solution(mesh):
    n_dp, n_col = mesh.devices.shape
    n_x = n_col
    grid = Mesh(mesh.devices.reshape(n_x, n_dp // n_x, n_col), ("x", "zc", "col"))
    rows = ("x", "zc")
    placed = (P(rows, None), P(None, "col"), P(rows, None), P(), P())
    return jax.shard_map(
        per_device, mesh=grid, in_specs=placed, out_specs=P("col", rows), check_vma=False
    )
```

```python
import functools

import jax
import jax.numpy as jnp
from jax import lax
from jax.experimental import pallas as pl
from jax.experimental.pallas import tpu as pltpu
from jax.sharding import Mesh, PartitionSpec as P

MESH = pl.DeviceIdType.MESH


def gather_kernel(n_x, n_z, stride, block_ref, cand_ref, slot_ref, out_ref, flags_ref, held, send_own,
                  recv_own, send_fwd, recv_fwd, send_x, recv_x, send_pair, recv_pair, own_sem):
    me_x = lax.axis_index("x")
    me_zc = lax.axis_index("zc")
    me_y = lax.axis_index("col")
    me_z = me_zc // 2
    lane = me_zc % 2
    pair = me_z * 2 + 1 - lane
    on_diagonal = me_x == me_y
    reach = (n_z // 2, (n_z - 1) // 2)
    near = tuple(min(stride, r) for r in reach)
    x_peers = [(k, lax.rem(me_x + k, n_x)) for k in range(1, n_x)]

    def along(way, hops):
        z = me_z + hops if way == 0 else me_z - hops
        return lax.rem(z + 2 * n_z, n_z) * 2 + lane

    barrier = pltpu.get_barrier_semaphore()
    peers = []
    for way in range(2):
        for k in range(1, near[way] + 1):
            peers += [(me_y, along(way, k), me_x), (me_y, along(way, -k), me_x)]
        if reach[way] > near[way]:
            peers += [(me_x, along(way, stride), me_y), (me_x, along(way, -stride), me_y)]
    peers += [(px, me_zc, me_y) for _, px in x_peers]
    peers.append((me_x, pair, me_y))
    for peer in peers:
        pl.semaphore_signal(barrier, inc=1, device_id=peer, device_id_type=MESH)

    @pl.when(jnp.logical_not(on_diagonal))
    def _():
        pl.semaphore_signal(barrier, inc=1, device_id=(me_y, me_zc, me_x), device_id_type=MESH)

    pl.semaphore_wait(barrier, len(peers) + jnp.where(on_diagonal, 0, 1))

    def own_copy(way, k):
        return pltpu.make_async_remote_copy(
            src_ref=block_ref, dst_ref=held.at[me_y, lane, me_z],
            send_sem=send_own.at[way, k], recv_sem=recv_own.at[way, k],
            device_id=(me_y, along(way, k), me_x), device_id_type=MESH)

    for k in range(1, max(near) + 1):
        for way in range(2):
            if k <= near[way]:
                own_copy(way, k).start()
    own = pltpu.make_async_copy(block_ref, held.at[me_x, lane, me_z], own_sem)

    @pl.when(on_diagonal)
    def _():
        own.start()

    @pl.when(jnp.logical_not(on_diagonal))
    def _():
        own_copy(0, 0).start()

    rows = flags_ref.shape[0]
    slots = slot_ref[...]
    number = lax.broadcasted_iota(jnp.int32, slots.shape, 0) * slots.shape[1]
    number = number + lax.broadcasted_iota(jnp.int32, slots.shape, 1)
    owner = jnp.sum(jnp.where(slots == me_x * (2 * n_z) + me_zc, number, 0), keepdims=True)
    listed = cand_ref[pl.ds(pl.multiple_of(me_y * rows, rows), rows), :] == owner
    flags_ref[...] = jnp.max(listed.astype(jnp.float32), axis=1, keepdims=True)

    @pl.when(on_diagonal)
    def _():
        own.wait()

    @pl.when(jnp.logical_not(on_diagonal))
    def _():
        pltpu.make_async_remote_copy(
            src_ref=block_ref, dst_ref=held.at[me_x, lane, me_z],
            send_sem=send_own.at[0, 0], recv_sem=recv_own.at[0, 0],
            device_id=(me_y, me_zc, me_x), device_id_type=MESH).wait_recv()

    def fwd_copy(way, hops, slot_z):
        line = held.at[me_x, lane, slot_z]
        return pltpu.make_async_remote_copy(
            src_ref=line, dst_ref=line, send_sem=send_fwd.at[way, hops + stride],
            recv_sem=recv_fwd.at[way, hops + stride],
            device_id=(me_x, along(way, stride), me_y), device_id_type=MESH)

    forwarded = []
    for hops in range(1, max(reach) + 1):
        for way in range(2):
            if hops > reach[way]:
                continue
            origin = along(way, -hops) // 2
            line = held.at[me_x, lane, origin]
            if hops <= near[way]:
                source, sems = (me_y, along(way, -hops), me_x), (send_own.at[way, hops], recv_own.at[way, hops])
            else:
                source, sems = (me_x, along(way, -stride), me_y), (send_fwd.at[way, hops], recv_fwd.at[way, hops])
            pltpu.make_async_remote_copy(
                src_ref=line, dst_ref=line, send_sem=sems[0], recv_sem=sems[1],
                device_id=source, device_id_type=MESH).wait_recv()
            if hops + stride <= reach[way]:
                fwd_copy(way, hops, origin).start()
                forwarded.append((way, hops, origin))

    def to_pair(c, index):
        line = held.at[c, lane]
        return pltpu.make_async_remote_copy(
            src_ref=line, dst_ref=line, send_sem=send_pair.at[index], recv_sem=recv_pair.at[index],
            device_id=(me_x, pair, me_y), device_id_type=MESH)

    def x_copy(k, px):
        line = held.at[me_x, lane]
        return pltpu.make_async_remote_copy(
            src_ref=line, dst_ref=line, send_sem=send_x.at[k], recv_sem=recv_x.at[n_x - k],
            device_id=(px, me_zc, me_y), device_id_type=MESH)

    to_pair(me_x, 0).start()
    for k, px in x_peers:
        x_copy(k, px).start()
    for k, px in x_peers:
        line = held.at[px, lane]
        pltpu.make_async_remote_copy(
            src_ref=line, dst_ref=line, send_sem=send_x.at[k], recv_sem=recv_x.at[k],
            device_id=(px, me_zc, me_y), device_id_type=MESH).wait_recv()
        to_pair(px, k).start()

    for index in range(n_x):
        c = me_x if index == 0 else x_peers[index - 1][1]
        line = held.at[c, 1 - lane]
        pltpu.make_async_remote_copy(
            src_ref=line, dst_ref=line, send_sem=send_pair.at[index], recv_sem=recv_pair.at[index],
            device_id=(me_x, pair, me_y), device_id_type=MESH).wait_recv()

    for way in range(2):
        for k in range(1, near[way] + 1):
            own_copy(way, k).wait_send()

    @pl.when(jnp.logical_not(on_diagonal))
    def _():
        own_copy(0, 0).wait_send()

    for way, hops, origin in forwarded:
        fwd_copy(way, hops, origin).wait_send()
    for k, px in x_peers:
        x_copy(k, px).wait_send()
    to_pair(me_x, 0).wait_send()
    for k, px in x_peers:
        to_pair(px, k).wait_send()
    out_ref[...] = held[...]


def gather_rows(block, candidates, block_slot, n_x, n_zc, rows):
    n_z = n_zc // 2
    stride = max(1, min(4, n_z // 4))
    shape = (n_x, 2, n_z) + block.shape
    slots = block_slot.reshape(-1, 128) if block_slot.size % 128 == 0 else block_slot.reshape(1, -1)
    return pl.pallas_call(
        functools.partial(gather_kernel, n_x, n_z, stride),
        out_shape=(
            jax.ShapeDtypeStruct(shape, block.dtype),
            jax.ShapeDtypeStruct((rows, 1), jnp.float32),
        ),
        in_specs=[pl.BlockSpec(memory_space=pltpu.VMEM)] * 3,
        out_specs=(pl.BlockSpec(memory_space=pltpu.VMEM), pl.BlockSpec(memory_space=pltpu.VMEM)),
        scratch_shapes=[
            pltpu.VMEM(shape, block.dtype),
            pltpu.SemaphoreType.DMA((2, stride + 1)),
            pltpu.SemaphoreType.DMA((2, stride + 1)),
            pltpu.SemaphoreType.DMA((2, n_z // 2 + 1)),
            pltpu.SemaphoreType.DMA((2, n_z // 2 + 1)),
            pltpu.SemaphoreType.DMA((n_x,)),
            pltpu.SemaphoreType.DMA((n_x,)),
            pltpu.SemaphoreType.DMA((n_x,)),
            pltpu.SemaphoreType.DMA((n_x,)),
            pltpu.SemaphoreType.DMA(()),
        ],
        compiler_params=pltpu.CompilerParams(collective_id=0, has_side_effects=True),
        cost_estimate=pl.CostEstimate(
            flops=0, transcendentals=0, bytes_accessed=2 * n_x * n_zc * block.size * 2
        ),
    )(block, candidates, slots)


def per_device(queries, kernel_inv, train_grads, candidates, block_slot):
    n_x = lax.axis_size("x")
    n_zc = lax.axis_size("zc")
    n_col = lax.axis_size("col")
    per_col = candidates.shape[0] // n_col
    precond = jnp.dot(queries, kernel_inv, preferred_element_type=jnp.float32).astype(jnp.bfloat16)
    rows, width = precond.shape
    tile = precond.reshape(rows * width // 128, 128)
    held, flags = gather_rows(tile, candidates, block_slot, n_x, n_zc, per_col)
    held = held.reshape(n_x, 2, n_zc // 2, rows, width // 128, 128)
    selected = jnp.transpose(held, (2, 1, 3, 0, 4, 5)).reshape(per_col, n_x * width)
    partial_scores = lax.dot_general(
        selected, train_grads, (((1,), (1,)), ((), ())), preferred_element_type=jnp.float32
    )
    return (partial_scores * flags).astype(jnp.bfloat16)


def solution(mesh):
    n_dp, n_col = mesh.devices.shape
    n_x = n_col
    grid = Mesh(mesh.devices.reshape(n_x, n_dp // n_x, n_col), ("x", "zc", "col"))
    rows = ("x", "zc")
    placed = (P(rows, None), P(None, "col"), P(rows, None), P(), P())
    return jax.shard_map(
        per_device, mesh=grid, in_specs=placed, out_specs=P("col", rows), check_vma=False
    )
```

```python
import functools

import jax
import jax.numpy as jnp
from jax import lax
from jax.experimental import pallas as pl
from jax.experimental.pallas import tpu as pltpu
from jax.sharding import Mesh, PartitionSpec as P

MESH = pl.DeviceIdType.MESH


def gather_kernel(n_x, n_z, stride, block_ref, cand_ref, slot_ref, out_ref, flags_ref, held, send_own,
                  recv_own, send_fwd, recv_fwd, send_x, recv_x, send_pair, recv_pair, own_sem):
    me_x = lax.axis_index("x")
    me_zc = lax.axis_index("zc")
    me_y = lax.axis_index("col")
    me_z = me_zc // 2
    lane = me_zc % 2
    pair = me_z * 2 + 1 - lane
    on_diagonal = me_x == me_y
    reach = (n_z // 2, (n_z - 1) // 2)
    near = tuple(min(stride, r) for r in reach)
    x_peers = [(k, lax.rem(me_x + k, n_x)) for k in range(1, n_x)]

    def along(way, hops):
        z = me_z + hops if way == 0 else me_z - hops
        return lax.rem(z + 2 * n_z, n_z) * 2 + lane

    barrier = pltpu.get_barrier_semaphore()
    peers = []
    for way in range(2):
        for k in range(1, near[way] + 1):
            peers += [(me_y, along(way, k), me_x), (me_y, along(way, -k), me_x)]
        if reach[way] > near[way]:
            peers += [(me_x, along(way, stride), me_y), (me_x, along(way, -stride), me_y)]
    peers += [(px, me_z * 2 + other, me_y) for _, px in x_peers for other in range(2)]
    peers.append((me_x, pair, me_y))
    for peer in peers:
        pl.semaphore_signal(barrier, inc=1, device_id=peer, device_id_type=MESH)

    @pl.when(jnp.logical_not(on_diagonal))
    def _():
        pl.semaphore_signal(barrier, inc=1, device_id=(me_y, me_zc, me_x), device_id_type=MESH)

    pl.semaphore_wait(barrier, len(peers) + jnp.where(on_diagonal, 0, 1))

    def own_copy(way, k):
        return pltpu.make_async_remote_copy(
            src_ref=block_ref, dst_ref=held.at[me_y, lane, me_z],
            send_sem=send_own.at[way, k], recv_sem=recv_own.at[way, k],
            device_id=(me_y, along(way, k), me_x), device_id_type=MESH)

    for k in range(1, max(near) + 1):
        for way in range(2):
            if k <= near[way]:
                own_copy(way, k).start()
    own = pltpu.make_async_copy(block_ref, held.at[me_x, lane, me_z], own_sem)

    @pl.when(on_diagonal)
    def _():
        own.start()

    @pl.when(jnp.logical_not(on_diagonal))
    def _():
        own_copy(0, 0).start()

    rows = flags_ref.shape[0]
    slots = slot_ref[...]
    number = lax.broadcasted_iota(jnp.int32, slots.shape, 0) * slots.shape[1]
    number = number + lax.broadcasted_iota(jnp.int32, slots.shape, 1)
    owner = jnp.sum(jnp.where(slots == me_x * (2 * n_z) + me_zc, number, 0), keepdims=True)
    listed = cand_ref[pl.ds(pl.multiple_of(me_y * rows, rows), rows), :] == owner
    flags_ref[...] = jnp.max(listed.astype(jnp.float32), axis=1, keepdims=True)

    def spread(slot_z):
        line = held.at[me_x, lane, slot_z]
        pltpu.make_async_remote_copy(
            src_ref=line, dst_ref=line, send_sem=send_pair, recv_sem=recv_pair,
            device_id=(me_x, pair, me_y), device_id_type=MESH).start()
        for k, px in x_peers:
            for other in range(2):
                pltpu.make_async_remote_copy(
                    src_ref=line, dst_ref=line, send_sem=send_x.at[k, other],
                    recv_sem=recv_x.at[n_x - k, lane],
                    device_id=(px, me_z * 2 + other, me_y), device_id_type=MESH).start()

    @pl.when(on_diagonal)
    def _():
        own.wait()

    @pl.when(jnp.logical_not(on_diagonal))
    def _():
        pltpu.make_async_remote_copy(
            src_ref=block_ref, dst_ref=held.at[me_x, lane, me_z],
            send_sem=send_own.at[0, 0], recv_sem=recv_own.at[0, 0],
            device_id=(me_y, me_zc, me_x), device_id_type=MESH).wait_recv()

    spread(me_z)

    def fwd_copy(way, hops, slot_z):
        line = held.at[me_x, lane, slot_z]
        return pltpu.make_async_remote_copy(
            src_ref=line, dst_ref=line, send_sem=send_fwd.at[way, hops + stride],
            recv_sem=recv_fwd.at[way, hops + stride],
            device_id=(me_x, along(way, stride), me_y), device_id_type=MESH)

    forwarded = []
    for hops in range(1, max(reach) + 1):
        for way in range(2):
            if hops > reach[way]:
                continue
            origin = along(way, -hops) // 2
            line = held.at[me_x, lane, origin]
            if hops <= near[way]:
                source, sems = (me_y, along(way, -hops), me_x), (send_own.at[way, hops], recv_own.at[way, hops])
            else:
                source, sems = (me_x, along(way, -stride), me_y), (send_fwd.at[way, hops], recv_fwd.at[way, hops])
            pltpu.make_async_remote_copy(
                src_ref=line, dst_ref=line, send_sem=sems[0], recv_sem=sems[1],
                device_id=source, device_id_type=MESH).wait_recv()
            if hops + stride <= reach[way]:
                fwd_copy(way, hops, origin).start()
                forwarded.append((way, hops, origin))
            spread(origin)

    for other_lane in range(2):
        for k, px in x_peers:
            line = held.at[px, other_lane]
            pltpu.make_async_remote_copy(
                src_ref=line, dst_ref=line, send_sem=send_x.at[k, other_lane],
                recv_sem=recv_x.at[k, other_lane],
                device_id=(px, me_z * 2 + other_lane, me_y), device_id_type=MESH).wait()
    line = held.at[me_x, 1 - lane]
    pltpu.make_async_remote_copy(
        src_ref=line, dst_ref=line, send_sem=send_pair, recv_sem=recv_pair,
        device_id=(me_x, pair, me_y), device_id_type=MESH).wait()

    for way in range(2):
        for k in range(1, near[way] + 1):
            own_copy(way, k).wait_send()

    @pl.when(jnp.logical_not(on_diagonal))
    def _():
        own_copy(0, 0).wait_send()

    for way, hops, origin in forwarded:
        fwd_copy(way, hops, origin).wait_send()
    out_ref[...] = held[...]


def gather_rows(block, candidates, block_slot, n_x, n_zc, rows):
    n_z = n_zc // 2
    stride = max(1, min(4, n_z // 4))
    shape = (n_x, 2, n_z) + block.shape
    slots = block_slot.reshape(-1, 128) if block_slot.size % 128 == 0 else block_slot.reshape(1, -1)
    return pl.pallas_call(
        functools.partial(gather_kernel, n_x, n_z, stride),
        out_shape=(
            jax.ShapeDtypeStruct(shape, block.dtype),
            jax.ShapeDtypeStruct((rows, 1), jnp.float32),
        ),
        in_specs=[pl.BlockSpec(memory_space=pltpu.VMEM)] * 3,
        out_specs=(pl.BlockSpec(memory_space=pltpu.VMEM), pl.BlockSpec(memory_space=pltpu.VMEM)),
        scratch_shapes=[
            pltpu.VMEM(shape, block.dtype),
            pltpu.SemaphoreType.DMA((2, stride + 1)),
            pltpu.SemaphoreType.DMA((2, stride + 1)),
            pltpu.SemaphoreType.DMA((2, n_z // 2 + 1)),
            pltpu.SemaphoreType.DMA((2, n_z // 2 + 1)),
            pltpu.SemaphoreType.DMA((n_x, 2)),
            pltpu.SemaphoreType.DMA((n_x, 2)),
            pltpu.SemaphoreType.DMA(()),
            pltpu.SemaphoreType.DMA(()),
            pltpu.SemaphoreType.DMA(()),
        ],
        compiler_params=pltpu.CompilerParams(collective_id=0, has_side_effects=True),
        cost_estimate=pl.CostEstimate(
            flops=0, transcendentals=0, bytes_accessed=2 * n_x * n_zc * block.size * 2
        ),
    )(block, candidates, slots)


def per_device(queries, kernel_inv, train_grads, candidates, block_slot):
    n_x = lax.axis_size("x")
    n_zc = lax.axis_size("zc")
    n_col = lax.axis_size("col")
    per_col = candidates.shape[0] // n_col
    precond = jnp.dot(queries, kernel_inv, preferred_element_type=jnp.float32).astype(jnp.bfloat16)
    rows, width = precond.shape
    tile = precond.reshape(rows * width // 128, 128)
    held, flags = gather_rows(tile, candidates, block_slot, n_x, n_zc, per_col)
    held = held.reshape(n_x, 2, n_zc // 2, rows, width // 128, 128)
    selected = jnp.transpose(held, (2, 1, 3, 0, 4, 5)).reshape(per_col, n_x * width)
    partial_scores = lax.dot_general(
        selected, train_grads, (((1,), (1,)), ((), ())), preferred_element_type=jnp.float32
    )
    return (partial_scores * flags).astype(jnp.bfloat16)


def solution(mesh):
    n_dp, n_col = mesh.devices.shape
    n_x = n_col
    grid = Mesh(mesh.devices.reshape(n_x, n_dp // n_x, n_col), ("x", "zc", "col"))
    rows = ("x", "zc")
    placed = (P(rows, None), P(None, "col"), P(rows, None), P(), P())
    return jax.shard_map(
        per_device, mesh=grid, in_specs=placed, out_specs=P("col", rows), check_vma=False
    )
```

```python
import functools

import jax
import jax.numpy as jnp
from jax import lax
from jax.experimental import pallas as pl
from jax.experimental.pallas import tpu as pltpu
from jax.sharding import Mesh, PartitionSpec as P

MESH = pl.DeviceIdType.MESH


def gather_kernel(n_x, n_z, stride, block_ref, cand_ref, slot_ref, out_ref, flags_ref, held, send_own,
                  recv_own, send_fwd, recv_fwd, send_x, recv_x, send_pair, recv_pair, own_sem):
    me_x = lax.axis_index("x")
    me_zc = lax.axis_index("zc")
    me_y = lax.axis_index("col")
    me_z = me_zc // 2
    lane = me_zc % 2
    pair = me_z * 2 + 1 - lane
    on_diagonal = me_x == me_y
    reach = (n_z // 2, (n_z - 1) // 2)
    near = tuple(min(stride, r) for r in reach)
    x_peers = [(k, lax.rem(me_x + k, n_x)) for k in range(1, n_x)]

    def along(way, hops):
        z = me_z + hops if way == 0 else me_z - hops
        return lax.rem(z + 2 * n_z, n_z) * 2 + lane

    barrier = pltpu.get_barrier_semaphore()
    peers = []
    for way in range(2):
        for k in range(1, near[way] + 1):
            peers += [(me_y, along(way, k), me_x), (me_y, along(way, -k), me_x)]
        if reach[way] > near[way]:
            peers += [(me_x, along(way, stride), me_y), (me_x, along(way, -stride), me_y)]
    peers += [(px, me_z * 2 + other, me_y) for _, px in x_peers for other in range(2)]
    peers.append((me_x, pair, me_y))
    for peer in peers:
        pl.semaphore_signal(barrier, inc=1, device_id=peer, device_id_type=MESH)

    @pl.when(jnp.logical_not(on_diagonal))
    def _():
        pl.semaphore_signal(barrier, inc=1, device_id=(me_y, me_zc, me_x), device_id_type=MESH)

    pl.semaphore_wait(barrier, len(peers) + jnp.where(on_diagonal, 0, 1))

    def own_copy(way, k):
        return pltpu.make_async_remote_copy(
            src_ref=block_ref, dst_ref=held.at[me_y, lane, me_z],
            send_sem=send_own.at[way, k], recv_sem=recv_own.at[way, k],
            device_id=(me_y, along(way, k), me_x), device_id_type=MESH)

    for k in range(1, max(near) + 1):
        for way in range(2):
            if k <= near[way]:
                own_copy(way, k).start()
    own = pltpu.make_async_copy(block_ref, held.at[me_x, lane, me_z], own_sem)

    @pl.when(on_diagonal)
    def _():
        own.start()

    @pl.when(jnp.logical_not(on_diagonal))
    def _():
        own_copy(0, 0).start()

    rows = flags_ref.shape[0]
    slots = slot_ref[...]
    number = lax.broadcasted_iota(jnp.int32, slots.shape, 0) * slots.shape[1]
    number = number + lax.broadcasted_iota(jnp.int32, slots.shape, 1)
    owner = jnp.sum(jnp.where(slots == me_x * (2 * n_z) + me_zc, number, 0), keepdims=True)
    listed = cand_ref[pl.ds(pl.multiple_of(me_y * rows, rows), rows), :] == owner
    flags_ref[...] = jnp.max(listed.astype(jnp.float32), axis=1, keepdims=True)

    def spread(slot_z):
        line = held.at[me_x, lane, slot_z]
        pltpu.make_async_remote_copy(
            src_ref=line, dst_ref=line, send_sem=send_pair, recv_sem=recv_pair,
            device_id=(me_x, pair, me_y), device_id_type=MESH).start()
        for k, px in x_peers:
            for other in range(2):
                pltpu.make_async_remote_copy(
                    src_ref=line, dst_ref=line, send_sem=send_x.at[k, other],
                    recv_sem=recv_x.at[n_x - k, lane],
                    device_id=(px, me_z * 2 + other, me_y), device_id_type=MESH).start()

    @pl.when(on_diagonal)
    def _():
        own.wait()

    @pl.when(jnp.logical_not(on_diagonal))
    def _():
        pltpu.make_async_remote_copy(
            src_ref=block_ref, dst_ref=held.at[me_x, lane, me_z],
            send_sem=send_own.at[0, 0], recv_sem=recv_own.at[0, 0],
            device_id=(me_y, me_zc, me_x), device_id_type=MESH).wait_recv()

    spread(me_z)

    def fwd_copy(way, hops, slot_z):
        line = held.at[me_x, lane, slot_z]
        return pltpu.make_async_remote_copy(
            src_ref=line, dst_ref=line, send_sem=send_fwd.at[way, hops + stride],
            recv_sem=recv_fwd.at[way, hops + stride],
            device_id=(me_x, along(way, stride), me_y), device_id_type=MESH)

    forwarded = []
    for hops in range(1, max(reach) + 1):
        for way in range(2):
            if hops > reach[way]:
                continue
            origin = along(way, -hops) // 2
            line = held.at[me_x, lane, origin]
            if hops <= near[way]:
                source, sems = (me_y, along(way, -hops), me_x), (send_own.at[way, hops], recv_own.at[way, hops])
            else:
                source, sems = (me_x, along(way, -stride), me_y), (send_fwd.at[way, hops], recv_fwd.at[way, hops])
            pltpu.make_async_remote_copy(
                src_ref=line, dst_ref=line, send_sem=sems[0], recv_sem=sems[1],
                device_id=source, device_id_type=MESH).wait_recv()
            if hops + stride <= reach[way]:
                fwd_copy(way, hops, origin).start()
                forwarded.append((way, hops, origin))
            spread(origin)

    for other_lane in range(2):
        for k, px in x_peers:
            line = held.at[px, other_lane]
            pltpu.make_async_remote_copy(
                src_ref=line, dst_ref=line, send_sem=send_x.at[k, other_lane],
                recv_sem=recv_x.at[k, other_lane],
                device_id=(px, me_z * 2 + other_lane, me_y), device_id_type=MESH).wait()
    line = held.at[me_x, 1 - lane]
    pltpu.make_async_remote_copy(
        src_ref=line, dst_ref=line, send_sem=send_pair, recv_sem=recv_pair,
        device_id=(me_x, pair, me_y), device_id_type=MESH).wait()

    for way in range(2):
        for k in range(1, near[way] + 1):
            own_copy(way, k).wait_send()

    @pl.when(jnp.logical_not(on_diagonal))
    def _():
        own_copy(0, 0).wait_send()

    for way, hops, origin in forwarded:
        fwd_copy(way, hops, origin).wait_send()
    out_ref[...] = held[...]


def gather_rows(block, candidates, block_slot, n_x, n_zc, rows):
    n_z = n_zc // 2
    stride = max(1, min(8, n_z // 4))
    shape = (n_x, 2, n_z) + block.shape
    slots = block_slot.reshape(-1, 128) if block_slot.size % 128 == 0 else block_slot.reshape(1, -1)
    return pl.pallas_call(
        functools.partial(gather_kernel, n_x, n_z, stride),
        out_shape=(
            jax.ShapeDtypeStruct(shape, block.dtype),
            jax.ShapeDtypeStruct((rows, 1), jnp.float32),
        ),
        in_specs=[pl.BlockSpec(memory_space=pltpu.VMEM)] * 3,
        out_specs=(pl.BlockSpec(memory_space=pltpu.VMEM), pl.BlockSpec(memory_space=pltpu.VMEM)),
        scratch_shapes=[
            pltpu.VMEM(shape, block.dtype),
            pltpu.SemaphoreType.DMA((2, stride + 1)),
            pltpu.SemaphoreType.DMA((2, stride + 1)),
            pltpu.SemaphoreType.DMA((2, n_z // 2 + 1)),
            pltpu.SemaphoreType.DMA((2, n_z // 2 + 1)),
            pltpu.SemaphoreType.DMA((n_x, 2)),
            pltpu.SemaphoreType.DMA((n_x, 2)),
            pltpu.SemaphoreType.DMA(()),
            pltpu.SemaphoreType.DMA(()),
            pltpu.SemaphoreType.DMA(()),
        ],
        compiler_params=pltpu.CompilerParams(collective_id=0, has_side_effects=True),
        cost_estimate=pl.CostEstimate(
            flops=0, transcendentals=0, bytes_accessed=2 * n_x * n_zc * block.size * 2
        ),
    )(block, candidates, slots)


def per_device(queries, kernel_inv, train_grads, candidates, block_slot):
    n_x = lax.axis_size("x")
    n_zc = lax.axis_size("zc")
    n_col = lax.axis_size("col")
    per_col = candidates.shape[0] // n_col
    precond = jnp.dot(queries, kernel_inv, preferred_element_type=jnp.float32).astype(jnp.bfloat16)
    rows, width = precond.shape
    tile = precond.reshape(rows * width // 128, 128)
    held, flags = gather_rows(tile, candidates, block_slot, n_x, n_zc, per_col)
    held = held.reshape(n_x, 2, n_zc // 2, rows, width // 128, 128)
    selected = jnp.transpose(held, (2, 1, 3, 0, 4, 5)).reshape(per_col, n_x * width)
    partial_scores = lax.dot_general(
        selected, train_grads, (((1,), (1,)), ((), ())), preferred_element_type=jnp.float32
    )
    return (partial_scores * flags).astype(jnp.bfloat16)


def solution(mesh):
    n_dp, n_col = mesh.devices.shape
    n_x = n_col
    grid = Mesh(mesh.devices.reshape(n_x, n_dp // n_x, n_col), ("x", "zc", "col"))
    rows = ("x", "zc")
    placed = (P(rows, None), P(None, "col"), P(rows, None), P(), P())
    return jax.shard_map(
        per_device, mesh=grid, in_specs=placed, out_specs=P("col", rows), check_vma=False
    )
```

```python
import functools

import jax
import jax.numpy as jnp
from jax import lax
from jax.experimental import pallas as pl
from jax.experimental.pallas import tpu as pltpu
from jax.sharding import Mesh, PartitionSpec as P

MESH = pl.DeviceIdType.MESH


def gather_kernel(n_x, n_z, stride, block_ref, cand_ref, slot_ref, out_ref, flags_ref, held, send_own,
                  recv_own, send_fwd, recv_fwd, send_x, recv_x, send_pair, recv_pair, send_fp, recv_fp,
                  own_sem):
    me_x = lax.axis_index("x")
    me_zc = lax.axis_index("zc")
    me_y = lax.axis_index("col")
    me_z = me_zc // 2
    lane = me_zc % 2
    pair = me_z * 2 + 1 - lane
    on_diagonal = me_x == me_y
    reach = (n_z // 2, (n_z - 1) // 2)
    near = tuple(min(stride, r) for r in reach)
    x_peers = [(k, lax.rem(me_x + k, n_x)) for k in range(1, n_x)]

    def along(way, hops):
        z = me_z + hops if way == 0 else me_z - hops
        return lax.rem(z + 2 * n_z, n_z) * 2 + lane

    barrier = pltpu.get_barrier_semaphore()
    peers = []
    for way in range(2):
        for k in range(1, near[way] + 1):
            peers += [(me_y, along(way, k), me_x), (me_y, along(way, -k), me_x)]
        if reach[way] > near[way]:
            peers += [(me_x, along(way, stride), me_y), (me_x, along(way, -stride), me_y)]
    peers += [(px, me_zc, me_y) for _, px in x_peers]
    peers.append((me_x, pair, me_y))
    for peer in peers:
        pl.semaphore_signal(barrier, inc=1, device_id=peer, device_id_type=MESH)

    @pl.when(jnp.logical_not(on_diagonal))
    def _():
        pl.semaphore_signal(barrier, inc=1, device_id=(me_y, me_zc, me_x), device_id_type=MESH)

    pl.semaphore_wait(barrier, len(peers) + jnp.where(on_diagonal, 0, 1))

    def own_copy(way, k):
        return pltpu.make_async_remote_copy(
            src_ref=block_ref, dst_ref=held.at[me_y, lane, me_z],
            send_sem=send_own.at[way, k], recv_sem=recv_own.at[way, k],
            device_id=(me_y, along(way, k), me_x), device_id_type=MESH)

    for k in range(1, max(near) + 1):
        for way in range(2):
            if k <= near[way]:
                own_copy(way, k).start()
    own = pltpu.make_async_copy(block_ref, held.at[me_x, lane, me_z], own_sem)

    @pl.when(on_diagonal)
    def _():
        own.start()

    @pl.when(jnp.logical_not(on_diagonal))
    def _():
        own_copy(0, 0).start()

    rows = flags_ref.shape[0]
    slots = slot_ref[...]
    number = lax.broadcasted_iota(jnp.int32, slots.shape, 0) * slots.shape[1]
    number = number + lax.broadcasted_iota(jnp.int32, slots.shape, 1)
    owner = jnp.sum(jnp.where(slots == me_x * (2 * n_z) + me_zc, number, 0), keepdims=True)
    listed = cand_ref[pl.ds(pl.multiple_of(me_y * rows, rows), rows), :] == owner
    flags_ref[...] = jnp.max(listed.astype(jnp.float32), axis=1, keepdims=True)

    def spread(slot_z):
        line = held.at[me_x, lane, slot_z]
        pltpu.make_async_remote_copy(
            src_ref=line, dst_ref=line, send_sem=send_pair, recv_sem=recv_pair,
            device_id=(me_x, pair, me_y), device_id_type=MESH).start()
        for k, px in x_peers:
            pltpu.make_async_remote_copy(
                src_ref=line, dst_ref=line, send_sem=send_x.at[k],
                recv_sem=recv_x.at[n_x - k, slot_z],
                device_id=(px, me_zc, me_y), device_id_type=MESH).start()

    @pl.when(on_diagonal)
    def _():
        own.wait()

    @pl.when(jnp.logical_not(on_diagonal))
    def _():
        pltpu.make_async_remote_copy(
            src_ref=block_ref, dst_ref=held.at[me_x, lane, me_z],
            send_sem=send_own.at[0, 0], recv_sem=recv_own.at[0, 0],
            device_id=(me_y, me_zc, me_x), device_id_type=MESH).wait_recv()

    spread(me_z)

    def fwd_copy(way, hops, slot_z):
        line = held.at[me_x, lane, slot_z]
        return pltpu.make_async_remote_copy(
            src_ref=line, dst_ref=line, send_sem=send_fwd.at[way, hops + stride],
            recv_sem=recv_fwd.at[way, hops + stride],
            device_id=(me_x, along(way, stride), me_y), device_id_type=MESH)

    forwarded = []
    origins = [me_z]
    for hops in range(1, max(reach) + 1):
        for way in range(2):
            if hops > reach[way]:
                continue
            origin = along(way, -hops) // 2
            line = held.at[me_x, lane, origin]
            if hops <= near[way]:
                source, sems = (me_y, along(way, -hops), me_x), (send_own.at[way, hops], recv_own.at[way, hops])
            else:
                source, sems = (me_x, along(way, -stride), me_y), (send_fwd.at[way, hops], recv_fwd.at[way, hops])
            pltpu.make_async_remote_copy(
                src_ref=line, dst_ref=line, send_sem=sems[0], recv_sem=sems[1],
                device_id=source, device_id_type=MESH).wait_recv()
            if hops + stride <= reach[way]:
                fwd_copy(way, hops, origin).start()
                forwarded.append((way, hops, origin))
            spread(origin)
            origins.append(origin)

    for origin in origins:
        for k, px in x_peers:
            line = held.at[px, lane, origin]
            pltpu.make_async_remote_copy(
                src_ref=line, dst_ref=line, send_sem=send_x.at[k], recv_sem=recv_x.at[k, origin],
                device_id=(px, me_zc, me_y), device_id_type=MESH).wait_recv()
            pltpu.make_async_remote_copy(
                src_ref=line, dst_ref=line, send_sem=send_fp.at[k], recv_sem=recv_fp.at[k],
                device_id=(me_x, pair, me_y), device_id_type=MESH).start()
    for k, px in x_peers:
        line = held.at[px, 1 - lane]
        pltpu.make_async_remote_copy(
            src_ref=line, dst_ref=line, send_sem=send_fp.at[k], recv_sem=recv_fp.at[k],
            device_id=(me_x, pair, me_y), device_id_type=MESH).wait()
        line = held.at[me_x, lane]
        pltpu.make_async_remote_copy(
            src_ref=line, dst_ref=line, send_sem=send_x.at[k], recv_sem=recv_x.at[n_x - k, 0],
            device_id=(px, me_zc, me_y), device_id_type=MESH).wait_send()
    line = held.at[me_x, 1 - lane]
    pltpu.make_async_remote_copy(
        src_ref=line, dst_ref=line, send_sem=send_pair, recv_sem=recv_pair,
        device_id=(me_x, pair, me_y), device_id_type=MESH).wait()

    for way in range(2):
        for k in range(1, near[way] + 1):
            own_copy(way, k).wait_send()

    @pl.when(jnp.logical_not(on_diagonal))
    def _():
        own_copy(0, 0).wait_send()

    for way, hops, origin in forwarded:
        fwd_copy(way, hops, origin).wait_send()
    out_ref[...] = held[...]


def gather_rows(block, candidates, block_slot, n_x, n_zc, rows):
    n_z = n_zc // 2
    stride = max(1, min(8, n_z // 4))
    shape = (n_x, 2, n_z) + block.shape
    slots = block_slot.reshape(-1, 128) if block_slot.size % 128 == 0 else block_slot.reshape(1, -1)
    return pl.pallas_call(
        functools.partial(gather_kernel, n_x, n_z, stride),
        out_shape=(
            jax.ShapeDtypeStruct(shape, block.dtype),
            jax.ShapeDtypeStruct((rows, 1), jnp.float32),
        ),
        in_specs=[pl.BlockSpec(memory_space=pltpu.VMEM)] * 3,
        out_specs=(pl.BlockSpec(memory_space=pltpu.VMEM), pl.BlockSpec(memory_space=pltpu.VMEM)),
        scratch_shapes=[
            pltpu.VMEM(shape, block.dtype),
            pltpu.SemaphoreType.DMA((2, stride + 1)),
            pltpu.SemaphoreType.DMA((2, stride + 1)),
            pltpu.SemaphoreType.DMA((2, n_z // 2 + 1)),
            pltpu.SemaphoreType.DMA((2, n_z // 2 + 1)),
            pltpu.SemaphoreType.DMA((n_x,)),
            pltpu.SemaphoreType.DMA((n_x, n_z)),
            pltpu.SemaphoreType.DMA(()),
            pltpu.SemaphoreType.DMA(()),
            pltpu.SemaphoreType.DMA((n_x,)),
            pltpu.SemaphoreType.DMA((n_x,)),
            pltpu.SemaphoreType.DMA(()),
        ],
        compiler_params=pltpu.CompilerParams(collective_id=0, has_side_effects=True),
        cost_estimate=pl.CostEstimate(
            flops=0, transcendentals=0, bytes_accessed=2 * n_x * n_zc * block.size * 2
        ),
    )(block, candidates, slots)


def per_device(queries, kernel_inv, train_grads, candidates, block_slot):
    n_x = lax.axis_size("x")
    n_zc = lax.axis_size("zc")
    n_col = lax.axis_size("col")
    per_col = candidates.shape[0] // n_col
    precond = jnp.dot(queries, kernel_inv, preferred_element_type=jnp.float32).astype(jnp.bfloat16)
    rows, width = precond.shape
    tile = precond.reshape(rows * width // 128, 128)
    held, flags = gather_rows(tile, candidates, block_slot, n_x, n_zc, per_col)
    held = held.reshape(n_x, 2, n_zc // 2, rows, width // 128, 128)
    selected = jnp.transpose(held, (2, 1, 3, 0, 4, 5)).reshape(per_col, n_x * width)
    partial_scores = lax.dot_general(
        selected, train_grads, (((1,), (1,)), ((), ())), preferred_element_type=jnp.float32
    )
    return (partial_scores * flags).astype(jnp.bfloat16)


def solution(mesh):
    n_dp, n_col = mesh.devices.shape
    n_x = n_col
    grid = Mesh(mesh.devices.reshape(n_x, n_dp // n_x, n_col), ("x", "zc", "col"))
    rows = ("x", "zc")
    placed = (P(rows, None), P(None, "col"), P(rows, None), P(), P())
    return jax.shard_map(
        per_device, mesh=grid, in_specs=placed, out_specs=P("col", rows), check_vma=False
    )
```

```python
import functools

import jax
import jax.numpy as jnp
from jax import lax
from jax.experimental import pallas as pl
from jax.experimental.pallas import tpu as pltpu
from jax.sharding import Mesh, PartitionSpec as P

MESH = pl.DeviceIdType.MESH


def gather_kernel(n_x, n_z, stride, block_ref, cand_ref, slot_ref, held, flags_ref, send_own,
                  recv_own, send_fwd, recv_fwd, send_x, recv_x, send_pair, recv_pair, own_sem):
    me_x = lax.axis_index("x")
    me_zc = lax.axis_index("zc")
    me_y = lax.axis_index("col")
    me_z = me_zc // 2
    lane = me_zc % 2
    pair = me_z * 2 + 1 - lane
    on_diagonal = me_x == me_y
    reach = (n_z // 2, (n_z - 1) // 2)
    near = tuple(min(stride, r) for r in reach)
    x_peers = [(k, lax.rem(me_x + k, n_x)) for k in range(1, n_x)]

    def along(way, hops):
        z = me_z + hops if way == 0 else me_z - hops
        return lax.rem(z + 2 * n_z, n_z) * 2 + lane

    barrier = pltpu.get_barrier_semaphore()
    peers = []
    for way in range(2):
        for k in range(1, near[way] + 1):
            peers += [(me_y, along(way, k), me_x), (me_y, along(way, -k), me_x)]
        if reach[way] > near[way]:
            peers += [(me_x, along(way, stride), me_y), (me_x, along(way, -stride), me_y)]
    peers += [(px, me_z * 2 + other, me_y) for _, px in x_peers for other in range(2)]
    peers.append((me_x, pair, me_y))
    for peer in peers:
        pl.semaphore_signal(barrier, inc=1, device_id=peer, device_id_type=MESH)

    @pl.when(jnp.logical_not(on_diagonal))
    def _():
        pl.semaphore_signal(barrier, inc=1, device_id=(me_y, me_zc, me_x), device_id_type=MESH)

    pl.semaphore_wait(barrier, len(peers) + jnp.where(on_diagonal, 0, 1))

    def own_copy(way, k):
        return pltpu.make_async_remote_copy(
            src_ref=block_ref, dst_ref=held.at[me_y, lane, me_z],
            send_sem=send_own.at[way, k], recv_sem=recv_own.at[way, k],
            device_id=(me_y, along(way, k), me_x), device_id_type=MESH)

    for k in range(1, max(near) + 1):
        for way in range(2):
            if k <= near[way]:
                own_copy(way, k).start()
    own = pltpu.make_async_copy(block_ref, held.at[me_x, lane, me_z], own_sem)

    @pl.when(on_diagonal)
    def _():
        own.start()

    @pl.when(jnp.logical_not(on_diagonal))
    def _():
        own_copy(0, 0).start()

    rows = flags_ref.shape[0]
    slots = slot_ref[...]
    number = lax.broadcasted_iota(jnp.int32, slots.shape, 0) * slots.shape[1]
    number = number + lax.broadcasted_iota(jnp.int32, slots.shape, 1)
    owner = jnp.sum(jnp.where(slots == me_x * (2 * n_z) + me_zc, number, 0), keepdims=True)
    listed = cand_ref[pl.ds(pl.multiple_of(me_y * rows, rows), rows), :] == owner
    flags_ref[...] = jnp.max(listed.astype(jnp.float32), axis=1, keepdims=True)

    def spread(slot_z):
        line = held.at[me_x, lane, slot_z]
        pltpu.make_async_remote_copy(
            src_ref=line, dst_ref=line, send_sem=send_pair, recv_sem=recv_pair,
            device_id=(me_x, pair, me_y), device_id_type=MESH).start()
        for k, px in x_peers:
            for other in range(2):
                pltpu.make_async_remote_copy(
                    src_ref=line, dst_ref=line, send_sem=send_x.at[k, other],
                    recv_sem=recv_x.at[n_x - k, lane],
                    device_id=(px, me_z * 2 + other, me_y), device_id_type=MESH).start()

    @pl.when(on_diagonal)
    def _():
        own.wait()

    @pl.when(jnp.logical_not(on_diagonal))
    def _():
        pltpu.make_async_remote_copy(
            src_ref=block_ref, dst_ref=held.at[me_x, lane, me_z],
            send_sem=send_own.at[0, 0], recv_sem=recv_own.at[0, 0],
            device_id=(me_y, me_zc, me_x), device_id_type=MESH).wait_recv()

    spread(me_z)

    def fwd_copy(way, hops, slot_z):
        line = held.at[me_x, lane, slot_z]
        return pltpu.make_async_remote_copy(
            src_ref=line, dst_ref=line, send_sem=send_fwd.at[way, hops + stride],
            recv_sem=recv_fwd.at[way, hops + stride],
            device_id=(me_x, along(way, stride), me_y), device_id_type=MESH)

    forwarded = []
    for hops in range(1, max(reach) + 1):
        for way in range(2):
            if hops > reach[way]:
                continue
            origin = along(way, -hops) // 2
            line = held.at[me_x, lane, origin]
            if hops <= near[way]:
                source, sems = (me_y, along(way, -hops), me_x), (send_own.at[way, hops], recv_own.at[way, hops])
            else:
                source, sems = (me_x, along(way, -stride), me_y), (send_fwd.at[way, hops], recv_fwd.at[way, hops])
            pltpu.make_async_remote_copy(
                src_ref=line, dst_ref=line, send_sem=sems[0], recv_sem=sems[1],
                device_id=source, device_id_type=MESH).wait_recv()
            if hops + stride <= reach[way]:
                fwd_copy(way, hops, origin).start()
                forwarded.append((way, hops, origin))
            spread(origin)

    for other_lane in range(2):
        for k, px in x_peers:
            line = held.at[px, other_lane]
            pltpu.make_async_remote_copy(
                src_ref=line, dst_ref=line, send_sem=send_x.at[k, other_lane],
                recv_sem=recv_x.at[k, other_lane],
                device_id=(px, me_z * 2 + other_lane, me_y), device_id_type=MESH).wait()
    line = held.at[me_x, 1 - lane]
    pltpu.make_async_remote_copy(
        src_ref=line, dst_ref=line, send_sem=send_pair, recv_sem=recv_pair,
        device_id=(me_x, pair, me_y), device_id_type=MESH).wait()

    for way in range(2):
        for k in range(1, near[way] + 1):
            own_copy(way, k).wait_send()

    @pl.when(jnp.logical_not(on_diagonal))
    def _():
        own_copy(0, 0).wait_send()

    for way, hops, origin in forwarded:
        fwd_copy(way, hops, origin).wait_send()


def gather_rows(block, candidates, block_slot, n_x, n_zc, rows):
    n_z = n_zc // 2
    stride = max(1, min(8, n_z // 4))
    shape = (n_x, 2, n_z) + block.shape
    slots = block_slot.reshape(-1, 128) if block_slot.size % 128 == 0 else block_slot.reshape(1, -1)
    return pl.pallas_call(
        functools.partial(gather_kernel, n_x, n_z, stride),
        out_shape=(
            jax.ShapeDtypeStruct(shape, block.dtype),
            jax.ShapeDtypeStruct((rows, 1), jnp.float32),
        ),
        in_specs=[pl.BlockSpec(memory_space=pltpu.VMEM)] * 3,
        out_specs=(pl.BlockSpec(memory_space=pltpu.VMEM), pl.BlockSpec(memory_space=pltpu.VMEM)),
        scratch_shapes=[
            pltpu.SemaphoreType.DMA((2, stride + 1)),
            pltpu.SemaphoreType.DMA((2, stride + 1)),
            pltpu.SemaphoreType.DMA((2, n_z // 2 + 1)),
            pltpu.SemaphoreType.DMA((2, n_z // 2 + 1)),
            pltpu.SemaphoreType.DMA((n_x, 2)),
            pltpu.SemaphoreType.DMA((n_x, 2)),
            pltpu.SemaphoreType.DMA(()),
            pltpu.SemaphoreType.DMA(()),
            pltpu.SemaphoreType.DMA(()),
        ],
        compiler_params=pltpu.CompilerParams(collective_id=0, has_side_effects=True),
        cost_estimate=pl.CostEstimate(
            flops=0, transcendentals=0, bytes_accessed=2 * n_x * n_zc * block.size * 2
        ),
    )(block, candidates, slots)


def per_device(queries, kernel_inv, train_grads, candidates, block_slot):
    n_x = lax.axis_size("x")
    n_zc = lax.axis_size("zc")
    n_col = lax.axis_size("col")
    per_col = candidates.shape[0] // n_col
    precond = jnp.dot(queries, kernel_inv, preferred_element_type=jnp.float32).astype(jnp.bfloat16)
    rows, width = precond.shape
    tile = precond.reshape(rows * width // 128, 128)
    held, flags = gather_rows(tile, candidates, block_slot, n_x, n_zc, per_col)
    held = held.reshape(n_x, 2, n_zc // 2, rows, width // 128, 128)
    selected = jnp.transpose(held, (2, 1, 3, 0, 4, 5)).reshape(per_col, n_x * width)
    partial_scores = lax.dot_general(
        selected, train_grads, (((1,), (1,)), ((), ())), preferred_element_type=jnp.float32
    )
    return (partial_scores * flags).astype(jnp.bfloat16)


def solution(mesh):
    n_dp, n_col = mesh.devices.shape
    n_x = n_col
    grid = Mesh(mesh.devices.reshape(n_x, n_dp // n_x, n_col), ("x", "zc", "col"))
    rows = ("x", "zc")
    placed = (P(rows, None), P(None, "col"), P(rows, None), P(), P())
    return jax.shard_map(
        per_device, mesh=grid, in_specs=placed, out_specs=P("col", rows), check_vma=False
    )
```

```python
import functools

import jax
import jax.numpy as jnp
from jax import lax
from jax.experimental import pallas as pl
from jax.experimental.pallas import tpu as pltpu
from jax.sharding import Mesh, PartitionSpec as P

MESH = pl.DeviceIdType.MESH


def gather_kernel(n_x, n_z, stride, block_ref, cand_ref, slot_ref, held, flags_ref, send_own,
                  recv_own, send_fwd, recv_fwd, send_x, recv_x, send_pair, recv_pair, own_sem):
    me_x = lax.axis_index("x")
    me_zc = lax.axis_index("zc")
    me_y = lax.axis_index("col")
    me_z = me_zc // 2
    lane = me_zc % 2
    pair = me_z * 2 + 1 - lane
    on_diagonal = me_x == me_y
    reach = (n_z // 2, (n_z - 1) // 2)
    near = tuple(min(stride, r) for r in reach)
    x_peers = [(k, lax.rem(me_x + k, n_x)) for k in range(1, n_x)]

    def along(way, hops):
        z = me_z + hops if way == 0 else me_z - hops
        return lax.rem(z + 2 * n_z, n_z) * 2 + lane

    barrier = pltpu.get_barrier_semaphore()
    peers = []
    for way in range(2):
        for k in range(1, near[way] + 1):
            peers += [(me_y, along(way, k), me_x), (me_y, along(way, -k), me_x)]
        if reach[way] > near[way]:
            peers += [(me_x, along(way, stride), me_y), (me_x, along(way, -stride), me_y)]
    peers += [(px, me_z * 2 + other, me_y) for _, px in x_peers for other in range(2)]
    peers.append((me_x, pair, me_y))
    for peer in peers:
        pl.semaphore_signal(barrier, inc=1, device_id=peer, device_id_type=MESH)

    @pl.when(jnp.logical_not(on_diagonal))
    def _():
        pl.semaphore_signal(barrier, inc=1, device_id=(me_y, me_zc, me_x), device_id_type=MESH)

    pl.semaphore_wait(barrier, len(peers) + jnp.where(on_diagonal, 0, 1))

    def own_copy(way, k):
        return pltpu.make_async_remote_copy(
            src_ref=block_ref, dst_ref=held.at[me_y, lane, me_z],
            send_sem=send_own.at[way, k], recv_sem=recv_own.at[way, k],
            device_id=(me_y, along(way, k), me_x), device_id_type=MESH)

    for k in range(1, max(near) + 1):
        for way in range(2):
            if k <= near[way]:
                own_copy(way, k).start()
    own = pltpu.make_async_copy(block_ref, held.at[me_x, lane, me_z], own_sem)

    @pl.when(on_diagonal)
    def _():
        own.start()

    @pl.when(jnp.logical_not(on_diagonal))
    def _():
        own_copy(0, 0).start()

    rows = flags_ref.shape[0]
    slots = slot_ref[...]
    number = lax.broadcasted_iota(jnp.int32, slots.shape, 0) * slots.shape[1]
    number = number + lax.broadcasted_iota(jnp.int32, slots.shape, 1)
    owner = jnp.sum(jnp.where(slots == me_x * (2 * n_z) + me_zc, number, 0), keepdims=True)
    listed = cand_ref[pl.ds(pl.multiple_of(me_y * rows, rows), rows), :] == owner
    flags_ref[...] = jnp.max(listed.astype(jnp.float32), axis=1, keepdims=True)

    def spread(slot_z):
        line = held.at[me_x, lane, slot_z]
        for k, px in x_peers:
            for other in range(2):
                pltpu.make_async_remote_copy(
                    src_ref=line, dst_ref=line, send_sem=send_x.at[k, other],
                    recv_sem=recv_x.at[n_x - k, lane],
                    device_id=(px, me_z * 2 + other, me_y), device_id_type=MESH).start()
        pltpu.make_async_remote_copy(
            src_ref=line, dst_ref=line, send_sem=send_pair, recv_sem=recv_pair,
            device_id=(me_x, pair, me_y), device_id_type=MESH).start()

    @pl.when(on_diagonal)
    def _():
        own.wait()

    @pl.when(jnp.logical_not(on_diagonal))
    def _():
        pltpu.make_async_remote_copy(
            src_ref=block_ref, dst_ref=held.at[me_x, lane, me_z],
            send_sem=send_own.at[0, 0], recv_sem=recv_own.at[0, 0],
            device_id=(me_y, me_zc, me_x), device_id_type=MESH).wait_recv()

    spread(me_z)

    def fwd_copy(way, hops, slot_z):
        line = held.at[me_x, lane, slot_z]
        return pltpu.make_async_remote_copy(
            src_ref=line, dst_ref=line, send_sem=send_fwd.at[way, hops + stride],
            recv_sem=recv_fwd.at[way, hops + stride],
            device_id=(me_x, along(way, stride), me_y), device_id_type=MESH)

    forwarded = []
    for hops in range(1, max(reach) + 1):
        for way in range(2):
            if hops > reach[way]:
                continue
            origin = along(way, -hops) // 2
            line = held.at[me_x, lane, origin]
            if hops <= near[way]:
                source, sems = (me_y, along(way, -hops), me_x), (send_own.at[way, hops], recv_own.at[way, hops])
            else:
                source, sems = (me_x, along(way, -stride), me_y), (send_fwd.at[way, hops], recv_fwd.at[way, hops])
            pltpu.make_async_remote_copy(
                src_ref=line, dst_ref=line, send_sem=sems[0], recv_sem=sems[1],
                device_id=source, device_id_type=MESH).wait_recv()
            if hops + stride <= reach[way]:
                fwd_copy(way, hops, origin).start()
                forwarded.append((way, hops, origin))
            spread(origin)

    for other_lane in range(2):
        for k, px in x_peers:
            line = held.at[px, other_lane]
            pltpu.make_async_remote_copy(
                src_ref=line, dst_ref=line, send_sem=send_x.at[k, other_lane],
                recv_sem=recv_x.at[k, other_lane],
                device_id=(px, me_z * 2 + other_lane, me_y), device_id_type=MESH).wait()
    line = held.at[me_x, 1 - lane]
    pltpu.make_async_remote_copy(
        src_ref=line, dst_ref=line, send_sem=send_pair, recv_sem=recv_pair,
        device_id=(me_x, pair, me_y), device_id_type=MESH).wait()

    for way in range(2):
        for k in range(1, near[way] + 1):
            own_copy(way, k).wait_send()

    @pl.when(jnp.logical_not(on_diagonal))
    def _():
        own_copy(0, 0).wait_send()

    for way, hops, origin in forwarded:
        fwd_copy(way, hops, origin).wait_send()


def gather_rows(block, candidates, block_slot, n_x, n_zc, rows):
    n_z = n_zc // 2
    stride = max(1, min(8, n_z // 4))
    shape = (n_x, 2, n_z) + block.shape
    slots = block_slot.reshape(-1, 128) if block_slot.size % 128 == 0 else block_slot.reshape(1, -1)
    return pl.pallas_call(
        functools.partial(gather_kernel, n_x, n_z, stride),
        out_shape=(
            jax.ShapeDtypeStruct(shape, block.dtype),
            jax.ShapeDtypeStruct((rows, 1), jnp.float32),
        ),
        in_specs=[pl.BlockSpec(memory_space=pltpu.VMEM)] * 3,
        out_specs=(pl.BlockSpec(memory_space=pltpu.VMEM), pl.BlockSpec(memory_space=pltpu.VMEM)),
        scratch_shapes=[
            pltpu.SemaphoreType.DMA((2, stride + 1)),
            pltpu.SemaphoreType.DMA((2, stride + 1)),
            pltpu.SemaphoreType.DMA((2, n_z // 2 + 1)),
            pltpu.SemaphoreType.DMA((2, n_z // 2 + 1)),
            pltpu.SemaphoreType.DMA((n_x, 2)),
            pltpu.SemaphoreType.DMA((n_x, 2)),
            pltpu.SemaphoreType.DMA(()),
            pltpu.SemaphoreType.DMA(()),
            pltpu.SemaphoreType.DMA(()),
        ],
        compiler_params=pltpu.CompilerParams(collective_id=0, has_side_effects=True),
        cost_estimate=pl.CostEstimate(
            flops=0, transcendentals=0, bytes_accessed=2 * n_x * n_zc * block.size * 2
        ),
    )(block, candidates, slots)


def per_device(queries, kernel_inv, train_grads, candidates, block_slot):
    n_x = lax.axis_size("x")
    n_zc = lax.axis_size("zc")
    n_col = lax.axis_size("col")
    per_col = candidates.shape[0] // n_col
    precond = jnp.dot(queries, kernel_inv, preferred_element_type=jnp.float32).astype(jnp.bfloat16)
    rows, width = precond.shape
    tile = precond.reshape(rows * width // 128, 128)
    held, flags = gather_rows(tile, candidates, block_slot, n_x, n_zc, per_col)
    held = held.reshape(n_x, 2, n_zc // 2, rows, width // 128, 128)
    selected = jnp.transpose(held, (2, 1, 3, 0, 4, 5)).reshape(per_col, n_x * width)
    partial_scores = lax.dot_general(
        selected, train_grads, (((1,), (1,)), ((), ())), preferred_element_type=jnp.float32
    )
    return (partial_scores * flags).astype(jnp.bfloat16)


def solution(mesh):
    n_dp, n_col = mesh.devices.shape
    n_x = n_col
    grid = Mesh(mesh.devices.reshape(n_x, n_dp // n_x, n_col), ("x", "zc", "col"))
    rows = ("x", "zc")
    placed = (P(rows, None), P(None, "col"), P(rows, None), P(), P())
    return jax.shard_map(
        per_device, mesh=grid, in_specs=placed, out_specs=P("col", rows), check_vma=False
    )
```
